32 devices in a mesh: dp: 8 (over z, y), fsdp: 4 (over x, core).
Axes of the slice: x: 2, y: 2, z: 4, core: 2. Of those that a mesh axis runs over, the one named last changes fastest.
Arguments:
- inputs: bfloat16 [2, 16384, 768], P(None, ('dp', 'fsdp')), may hold values from -6 to 6
- cotangent: bfloat16 [2, 16384, 768], P(None, ('dp', 'fsdp')), may hold values from -6 to 6
- prefix: int32 [2, 16], P(None, 'dp'), may hold values from 102 to 512, as said below
- w_query: bfloat16 [768, 768], P(('dp', 'fsdp')), may hold values from -0.21875 to 0.21875
- w_key: bfloat16 [768, 768], P(('dp', 'fsdp')), may hold values from -0.21875 to 0.21875
- w_value: bfloat16 [768, 768], P(('dp', 'fsdp')), may hold values from -0.21875 to 0.21875
- w_out: bfloat16 [768, 768], P(('dp', 'fsdp')), may hold values from -0.875 to 0.875
- w_up: bfloat16 [768, 3072], P(('dp', 'fsdp')), may hold values from -0.21875 to 0.21875
- w_down: bfloat16 [3072, 768], P(('dp', 'fsdp')), may hold values from -0.109375 to 0.109375
- b_query: bfloat16 [768], P(('dp', 'fsdp')), may hold values from -1.796875 to 1.796875
- b_value: bfloat16 [768], P(('dp', 'fsdp')), may hold values from -1.796875 to 1.796875
- b_out: bfloat16 [768], P(('dp', 'fsdp')), may hold values from -1.796875 to 1.796875
- b_up: bfloat16 [3072], P(('dp', 'fsdp')), may hold values from -1.796875 to 1.796875
- b_down: bfloat16 [768], P(('dp', 'fsdp')), may hold values from -1.796875 to 1.796875
- gain_attn: bfloat16 [768], P(('dp', 'fsdp')), may hold values from 0.5 to 1.5
- shift_attn: bfloat16 [768], P(('dp', 'fsdp')), may hold values from -1.796875 to 1.796875
- gain_ffn: bfloat16 [768], P(('dp', 'fsdp')), may hold values from 0.5 to 1.5
- shift_ffn: bfloat16 [768], P(('dp', 'fsdp')), may hold values from -1.796875 to 1.796875
Outputs:
- layer_out: bfloat16 [2, 16384, 768], P(None, ('dp', 'fsdp'))
- grad_inputs: float32 [2, 16384, 768], P(None, ('dp', 'fsdp'))
- grad_w_query: float32 [768, 768], P(('dp', 'fsdp'))
- grad_w_key: float32 [768, 768], P(('dp', 'fsdp'))
- grad_w_value: float32 [768, 768], P(('dp', 'fsdp'))
- grad_w_out: float32 [768, 768], P(('dp', 'fsdp'))
- grad_w_up: float32 [768, 3072], P(('dp', 'fsdp'))
- grad_w_down: float32 [3072, 768], P(('dp', 'fsdp'))
- grad_b_query: float32 [768], P(('dp', 'fsdp'))
- grad_b_value: float32 [768], P(('dp', 'fsdp'))
- grad_b_out: float32 [768], P(('dp', 'fsdp'))
- grad_b_up: float32 [3072], P(('dp', 'fsdp'))
- grad_b_down: float32 [768], P(('dp', 'fsdp'))
- grad_gain_attn: float32 [768], P(('dp', 'fsdp'))
- grad_shift_attn: float32 [768], P(('dp', 'fsdp'))
- grad_gain_ffn: float32 [768], P(('dp', 'fsdp'))
- grad_shift_ffn: float32 [768], P(('dp', 'fsdp'))
The draws below stay inside these ranges and needn't reach their ends.
Inputs may be any that keep to these rules, and one draw needn't show every extreme that they name: The bidirectional prefix of sequence s in micro-batch m; it never passes 1024 // 2, so block 1 of every sequence is causal.
All inputs are finite; a program needn't handle non-finite values.
Results may differ from the reference program's by a relative error of at most 0.015.
Values may be sent and summed in bfloat16 or wider, within the bound.
No kernel may reach another device: no remote copies, remote signals or barrier semaphores. Data moves between devices by JAX's collectives and lax.ppermute only.
A program may use at most 256 MiB of HBM per device.

```python
from functools import partial
import jax
import jax.numpy as jnp
from jax import lax

D = 768
FF = 3072
HEADS = 12
HEAD_DIM = 64
BLOCK = 512
GLOBAL = 128
MICRO = 2
SEQS = 16
TOKENS = 16384


def draw_prefix(key, part):
    lowest = 2 * BLOCK // 10
    highest_len = 2 * BLOCK // 2
    base = jax.random.randint(key, (MICRO, SEQS), lowest, highest_len + 1).astype(jnp.int32)
    base = base.at[0, 0].set(highest_len)
    return base.at[0, 1].set(lowest)


def levels(own_key, shape, cuts, least, top_value):
    level, own = 1.0, jax.random.fold_in(own_key, 6)
    for position, shards_of in cuts:
        steps = jnp.exp(jax.random.uniform(jax.random.fold_in(own, position), (shards_of,), jnp.float32, least / len(cuts), top_value / len(cuts)))
        level = level * jnp.repeat(steps, shape[position] // shards_of).reshape([-1 if axis == position else 1 for axis in range(len(shape))])
    return level


def normal_values(key, shape, deviation, bound, cuts=(), held_as=jnp.bfloat16):
    level = levels(key, shape, cuts, -0.22, 0.18) if cuts else 1.0
    array = jax.random.normal(key, shape, jnp.float32) * deviation * level
    return jnp.minimum(jnp.maximum(array, -bound), bound).astype(held_as)


def setup_inputs(seed: int = 0) -> dict:
    seeds = jax.random.split(jax.random.key(seed), 19)
    return {
        "inputs": normal_values(seeds[0], (MICRO, TOKENS, D), 1.0, 6.0, ((1, 32),)),
        "cotangent": normal_values(seeds[1], (MICRO, TOKENS, D), 1.0, 6.0, ((1, 32),)),
        "prefix": draw_prefix(jax.random.fold_in(seeds[18], 71), 0),
        "w_query": normal_values(seeds[3], (D, D), D ** -0.5, 0.21875, ((0, 32),)),
        "w_key": normal_values(seeds[4], (D, D), D ** -0.5, 0.21875, ((0, 32),)),
        "w_value": normal_values(seeds[5], (D, D), D ** -0.5, 0.21875, ((0, 32),)),
        "w_out": normal_values(seeds[6], (D, D), (D // 16) ** -0.5, 0.875, ((0, 32),)),
        "w_up": normal_values(seeds[7], (D, FF), D ** -0.5, 0.21875, ((0, 32),)),
        "w_down": normal_values(seeds[8], (FF, D), FF ** -0.5, 0.109375, ((0, 32),)),
        "b_query": normal_values(seeds[9], (D,), 0.3, 1.796875, ((0, 32),)),
        "b_value": normal_values(seeds[10], (D,), 0.3, 1.796875, ((0, 32),)),
        "b_out": normal_values(seeds[11], (D,), 0.3, 1.796875, ((0, 32),)),
        "b_up": normal_values(seeds[12], (FF,), 0.3, 1.796875, ((0, 32),)),
        "b_down": normal_values(seeds[13], (D,), 0.3, 1.796875, ((0, 32),)),
        "gain_attn": jnp.clip(1.0 + 0.1 * jax.random.normal(seeds[14], (D,), jnp.float32), 0.5, 1.5).astype(jnp.bfloat16),
        "shift_attn": normal_values(seeds[15], (D,), 0.3, 1.796875, ((0, 32),)),
        "gain_ffn": jnp.clip(1.0 + 0.1 * jax.random.normal(seeds[16], (D,), jnp.float32), 0.5, 1.5).astype(jnp.bfloat16),
        "shift_ffn": normal_values(seeds[17], (D,), 0.3, 1.796875, ((0, 32),)),
    }


norm_epsilon = 1e-05
score_scale = 0.125
masked_fill = -1e+30
highest = lax.Precision.HIGHEST

@jax.custom_vjp
def low(v):
    return lax.optimization_barrier(v.astype(jnp.bfloat16)).astype(jnp.float32)

@jax.custom_vjp
def low_back(v):
    return v

def low_keep(v):
    return (low(v), None)

def low_pass(kept, grad):
    return (grad,)

def back_keep(v):
    return (v, None)

def back_low(kept, grad):
    return (low(grad),)
low.defvjp(low_keep, low_pass)
low_back.defvjp(back_keep, back_low)

def matmul(left, right):
    return jnp.einsum('btd,de->bte', left, right, precision=highest)

def layer_norm(values, gain, shift):
    center = lax.optimization_barrier(jnp.mean(values, -1, keepdims=True))
    centered = values - center
    spread = lax.optimization_barrier(jnp.mean(centered * centered, -1, keepdims=True))
    return centered * lax.rsqrt(spread + norm_epsilon) * gain + shift

def block_attend(queries, key_rows, value_rows, prefix_len, first_block):
    raw_scores = low_back(jnp.einsum('bqhd,bkhd->bhqk', queries, key_rows, precision=highest))
    scores = raw_scores * score_scale
    query_pos = jnp.arange(queries.shape[1]).astype(jnp.int32)[:, None]
    key_pos = jnp.arange(key_rows.shape[1]).astype(jnp.int32)[None, :] - GLOBAL
    if first_block:
        local = (key_pos <= query_pos)[None] | (key_pos[None] < prefix_len.astype(jnp.int32)[:, None, None])
        allowed = jnp.where(key_pos[None] < 0, False, local)
    else:
        allowed = jnp.where(key_pos < 0, True, key_pos <= query_pos)[None]
    scores = jnp.where(allowed[:, None], scores, masked_fill)
    row_top = lax.optimization_barrier(jnp.max(scores, -1, keepdims=True))
    expon = jnp.exp(scores - row_top)
    prob_rows = expon / lax.optimization_barrier(jnp.sum(expon, -1, keepdims=True))
    return jnp.einsum('bhqk,bkhd->bqhd', low(prob_rows), value_rows, precision=highest)

def attend(queries, key_all, value_all, prefix_len):
    batch = queries.shape[0]
    query_heads = queries.reshape(batch, 2 * BLOCK, HEADS, HEAD_DIM)
    key_heads = key_all.reshape(batch, 2 * BLOCK, HEADS, HEAD_DIM)
    value_heads = value_all.reshape(batch, 2 * BLOCK, HEADS, HEAD_DIM)
    pieces = []
    for block_num in range(2):
        lower = block_num * BLOCK
        key_rows = jnp.concatenate([key_heads[:, :GLOBAL], key_heads[:, lower:lower + BLOCK]], 1)
        value_rows = jnp.concatenate([value_heads[:, :GLOBAL], value_heads[:, lower:lower + BLOCK]], 1)
        attend_block = jax.checkpoint(partial(block_attend, first_block=block_num == 0))
        pieces.append(attend_block(query_heads[:, lower:lower + BLOCK], key_rows, value_rows, prefix_len))
    return jnp.concatenate(pieces, 1).reshape(batch, 2 * BLOCK, HEADS * HEAD_DIM)

def forward(params, values, prefix_len):
    w_query, w_key, w_value, w_out, w_up, w_down, b_query, b_value, b_out, b_up, b_down, gain_attn, shift_attn, gain_ffn, shift_ffn = params
    normed_one = low(layer_norm(values, gain_attn, shift_attn))
    queries = low(low_back(matmul(normed_one, w_query) + b_query))
    key_all = low(low_back(matmul(normed_one, w_key)))
    value_all = low(low_back(matmul(normed_one, w_value) + b_value))
    attended = low(low_back(attend(queries, key_all, value_all, prefix_len)))
    branch = low_back(matmul(attended, w_out) + b_out)
    middle = values + branch
    normed_two = low(layer_norm(middle, gain_ffn, shift_ffn))
    hidden = low_back(matmul(normed_two, w_up) + b_up)
    activated = low(jax.nn.gelu(hidden))
    feed = low_back(matmul(activated, w_down) + b_down)
    return middle + feed

def reference(inputs, cotangent, prefix, w_query, w_key, w_value, w_out, w_up, w_down, b_query, b_value, b_out, b_up, b_down, gain_attn, shift_attn, gain_ffn, shift_ffn):
    params = (w_query.astype(jnp.float32), w_key.astype(jnp.float32), w_value.astype(jnp.float32), w_out.astype(jnp.float32), w_up.astype(jnp.float32), w_down.astype(jnp.float32), b_query.astype(jnp.float32), b_value.astype(jnp.float32), b_out.astype(jnp.float32), b_up.astype(jnp.float32), b_down.astype(jnp.float32), gain_attn.astype(jnp.float32), shift_attn.astype(jnp.float32), gain_ffn.astype(jnp.float32), shift_ffn.astype(jnp.float32))
    steps_all = MICRO * SEQS // 4
    seq_len = 2 * BLOCK
    values_all = inputs.astype(jnp.float32).reshape(steps_all, 4, seq_len, D)
    cot_all = cotangent.astype(jnp.float32).reshape(steps_all, 4, seq_len, D)
    prefix_all = prefix.reshape(steps_all, 4)

    def step(grad_sum, item):
        values, cot_rows, prefix_rows = item
        result, pull = jax.vjp(lambda prm, val: forward(prm, val, prefix_rows), params, values)
        grad_params, grad_values = pull(cot_rows)
        grad_sum = jax.tree.map(lambda first, second: first + second, grad_sum, grad_params)
        return (grad_sum, (result.astype(jnp.bfloat16), grad_values))
    zero_grads = tuple((jnp.zeros(prm.shape, jnp.float32) for prm in params))
    grads, (results, grad_values) = lax.scan(step, zero_grads, (values_all, cot_all, prefix_all))
    layer_out = results.reshape(MICRO, SEQS * seq_len, D)
    grad_inputs = grad_values.reshape(MICRO, SEQS * seq_len, D)
    return (layer_out, grad_inputs, grads[0], grads[1], grads[2], grads[3], grads[4], grads[5], grads[6], grads[7], grads[8], grads[9], grads[10], grads[11], grads[12], grads[13], grads[14])
```

```python
import functools

import jax
import jax.numpy as jnp
from jax import lax
from jax.experimental import pallas as pl
from jax.experimental.pallas import tpu as pltpu
from jax.sharding import PartitionSpec as P

D = 768
FF = 3072
HEADS = 12
GLOBAL = 128
PAIR = 128

norm_epsilon = 1e-05
score_scale = 0.125
log2_e = 1.4426950408889634
masked_fill = -1e30
BOTH = ("dp", "fsdp")
f32 = jnp.float32
bf16 = jnp.bfloat16


def product(left, right):
    return jnp.dot(left, right, preferred_element_type=f32)


def product_t(left, right):
    return lax.dot_general(left, right, (((1,), (1,)), ((), ())), preferred_element_type=f32)


def product_w(left, right):
    return lax.dot_general(left, right, (((0,), (0,)), ((), ())), preferred_element_type=f32)


def normalize(values, gain, shift):
    center = jnp.mean(values, -1, keepdims=True)
    centered = values - center
    spread = jnp.mean(centered * centered, -1, keepdims=True)
    inv_std = lax.rsqrt(spread + norm_epsilon)
    normed = centered * inv_std
    return (normed * gain + shift, normed, inv_std)


def normalize_back(grad_out, normed, inv_std, gain):
    grad_norm = grad_out * gain
    return inv_std * (
        grad_norm
        - jnp.mean(grad_norm, -1, keepdims=True)
        - normed * jnp.mean(grad_norm * normed, -1, keepdims=True)
    )


def lane_half(shape):
    return lax.broadcasted_iota(jnp.int32, shape, 1) < 64


def attend_kernel(info, q_ref, k_ref, v_ref, lk_ref, lv_ref, out_ref, prob_ref, bias_ref):
    micro = pl.program_id(0)
    rows = q_ref.shape[0]

    @pl.when(pl.program_id(1) == 0)
    def _():
        first = info[0] == 1
        prefix_len = jnp.where(first, info[1 + micro], 0)
        query_pos = lax.broadcasted_iota(jnp.int32, (rows, rows), 0)
        key_pos = lax.broadcasted_iota(jnp.int32, (rows, rows), 1)
        allowed = (key_pos <= query_pos) | (key_pos < prefix_len)
        bias_ref[:, GLOBAL:] = jnp.where(allowed, 0.0, masked_fill)
        bias_ref[:, :GLOBAL] = jnp.full((rows, GLOBAL), jnp.where(first, masked_fill, 0.0), f32)

    queries = q_ref[...]
    keys = jnp.concatenate([lk_ref[...], k_ref[...]], 0)
    values = jnp.concatenate([lv_ref[...], v_ref[...]], 0)
    half = lane_half(queries.shape)
    outs = []
    for head in range(2):
        mine = half if head == 0 else jnp.logical_not(half)
        raw = product_t(jnp.where(mine, queries, jnp.zeros_like(queries)), keys)
        scores = raw * (score_scale * log2_e) + bias_ref[...]
        top = jnp.max(scores, -1, keepdims=True)
        expon = jnp.exp2(scores - top)
        total = jnp.sum(expon, -1, keepdims=True)
        prob = (expon * (1.0 / total)).astype(bf16)
        prob_ref[0, head] = prob
        outs.append(product(prob, values))
    out_ref[...] = jnp.where(half, outs[0], outs[1]).astype(bf16)


def attend_back_kernel(
    q_ref, k_ref, v_ref, lk_ref, lv_ref, g_ref, o_ref, prob_ref,
    dq_ref, dk_ref, dv_ref, lead_k_ref, lead_v_ref,
):
    queries = q_ref[...]
    grads = g_ref[...]
    keys = jnp.concatenate([lk_ref[...], k_ref[...]], 0)
    values = jnp.concatenate([lv_ref[...], v_ref[...]], 0)
    half = lane_half(queries.shape)
    half_k = lane_half(keys.shape)
    dot_all = grads.astype(f32) * o_ref[...].astype(f32)
    d_query, d_key, d_value = [], [], []
    for head in range(2):
        mine = half if head == 0 else jnp.logical_not(half)
        grad_head = jnp.where(mine, grads, jnp.zeros_like(grads))
        prob = prob_ref[0, head]
        delta = jnp.sum(jnp.where(mine, dot_all, 0.0), -1, keepdims=True)
        grad_prob = product_t(grad_head, values)
        grad_raw = (prob.astype(f32) * ((grad_prob - delta) * score_scale)).astype(bf16)
        d_query.append(product(grad_raw, keys))
        d_key.append(product_w(grad_raw, queries))
        d_value.append(product_w(prob, grads))
    dq_ref[...] = jnp.where(half, d_query[0], d_query[1]).astype(bf16)
    d_keys = jnp.where(half_k, d_key[0], d_key[1])
    d_values = jnp.where(half_k, d_value[0], d_value[1])
    dk_ref[...] = d_keys[GLOBAL:]
    dv_ref[...] = d_values[GLOBAL:]
    lead_k_ref[...] = d_keys[:GLOBAL].astype(bf16)
    lead_v_ref[...] = d_values[:GLOBAL].astype(bf16)


def attend(info, queries, keys, values, lead, micro, rows):
    pairs = D // PAIR
    tile = lambda m, p, *_: (m, p)
    shifted_tile = lambda m, p, *_: (m, p + pairs)
    row_spec = pl.BlockSpec((rows, PAIR), tile)
    return pl.pallas_call(
        attend_kernel,
        out_shape=(
            jax.ShapeDtypeStruct(queries.shape, bf16),
            jax.ShapeDtypeStruct((micro, HEADS, rows, GLOBAL + rows), bf16),
        ),
        grid_spec=pltpu.PrefetchScalarGridSpec(
            num_scalar_prefetch=1,
            grid=(micro, pairs),
            in_specs=[
                row_spec,
                row_spec,
                row_spec,
                pl.BlockSpec((GLOBAL, PAIR), tile),
                pl.BlockSpec((GLOBAL, PAIR), shifted_tile),
            ],
            out_specs=[
                row_spec,
                pl.BlockSpec((1, 2, rows, GLOBAL + rows), lambda m, p, *_: (m, p, 0, 0)),
            ],
            scratch_shapes=[pltpu.VMEM((rows, GLOBAL + rows), f32)],
        ),
        compiler_params=pltpu.CompilerParams(vmem_limit_bytes=48 << 20),
        name="attend",
    )(info, queries, keys, values, lead, lead)


def attend_back(queries, keys, values, lead, grads, attended, probs, micro, rows):
    pairs = D // PAIR
    tile = lambda m, p: (m, p)
    shifted_tile = lambda m, p: (m, p + pairs)
    row_spec = pl.BlockSpec((rows, PAIR), tile)
    lead_spec = pl.BlockSpec((GLOBAL, PAIR), tile)
    full = queries.shape
    return pl.pallas_call(
        attend_back_kernel,
        out_shape=(
            jax.ShapeDtypeStruct(full, bf16),
            jax.ShapeDtypeStruct(full, f32),
            jax.ShapeDtypeStruct(full, f32),
            jax.ShapeDtypeStruct((micro * GLOBAL, D), bf16),
            jax.ShapeDtypeStruct((micro * GLOBAL, D), bf16),
        ),
        grid=(micro, pairs),
        in_specs=[
            row_spec,
            row_spec,
            row_spec,
            lead_spec,
            pl.BlockSpec((GLOBAL, PAIR), shifted_tile),
            row_spec,
            row_spec,
            pl.BlockSpec((1, 2, rows, GLOBAL + rows), lambda m, p: (m, p, 0, 0)),
        ],
        out_specs=[row_spec, row_spec, row_spec, lead_spec, lead_spec],
        compiler_params=pltpu.CompilerParams(vmem_limit_bytes=48 << 20),
        name="attend_back",
    )(queries, keys, values, lead, lead, grads, attended, probs)


def bits_of(count):
    assert count & (count - 1) == 0
    return count.bit_length() - 1


def swap(value, axis, bit):
    count = lax.axis_size(axis)
    return lax.ppermute(value, axis, [(i, i ^ (1 << bit)) for i in range(count)])


def stage_orders():
    along_f = [("fsdp", b) for b in range(bits_of(lax.axis_size("fsdp")))]
    along_d = [("dp", b) for b in range(bits_of(lax.axis_size("dp")))]
    order_a = along_f + along_d
    order_b = along_f[:1] + along_d[:1] + along_f[1:] + along_d[1:]
    return order_a, order_b


def scatter_sum(terms, order):
    rows, columns = terms.shape[1:]
    bits_f, bits_d = bits_of(lax.axis_size("fsdp")), bits_of(lax.axis_size("dp"))
    names = [("dp", b) for b in reversed(range(bits_d))] + [
        ("fsdp", b) for b in reversed(range(bits_f))
    ]
    held = terms.reshape((2,) * len(names) + (rows, columns))
    for stage in order:
        axis = names.index(stage)
        own = (lax.axis_index(stage[0]) >> stage[1]) & 1
        away = lax.dynamic_index_in_dim(held, 1 - own, axis, keepdims=False).astype(bf16)
        kept = lax.dynamic_index_in_dim(held, own, axis, keepdims=False)
        names = names[:axis] + names[axis + 1 :]
        held = kept + swap(away, *stage).astype(f32)
    return held


def spread_sum(value, order):
    for stage in order:
        value = value + swap(value, *stage)
    return value


def body(
    inputs, cotangent, prefix,
    w_query, w_key, w_value, w_out, w_up, w_down,
    b_query, b_value, b_out, b_up, b_down,
    gain_attn, shift_attn, gain_ffn, shift_ffn,
):
    n_dev = lax.axis_size("dp") * lax.axis_size("fsdp")
    share = w_query.shape[0]
    wide = FF // D
    fsdp_index = lax.axis_index("fsdp")
    own = lax.axis_index("dp") * lax.axis_size("fsdp") + fsdp_index
    first_block = fsdp_index % 2 == 0
    seq_slot = fsdp_index // 2
    micro, rows = inputs.shape[:2]

    vectors = (b_query, b_value, b_out, b_down, gain_attn, shift_attn, gain_ffn, shift_ffn, b_up)
    small = jnp.concatenate(vectors)
    small = jnp.pad(small[None], ((0, 7), (0, D - small.shape[0])))
    pack_one = jnp.concatenate([w_query, w_key, w_value, small], 0)
    pack_two = jnp.concatenate(
        [w_out] + [w_up[:, c * D : (c + 1) * D] for c in range(wide)] + [w_down], 0
    )
    got_one = lax.all_gather(pack_one, BOTH, axis=0)
    got_two = lax.all_gather(pack_two, BOTH, axis=0)

    def unit(got, at):
        return got[:, at * share : (at + 1) * share].reshape(D, D)

    full_query, full_key, full_value = (unit(got_one, i) for i in range(3))
    small_all = got_one[:, 3 * share].astype(f32)
    vector = lambda i: small_all[:, i * share : (i + 1) * share].reshape(D)
    bias_query, bias_value, bias_out, bias_down, gain_one, shift_one, gain_two, shift_two = (
        vector(i) for i in range(8)
    )
    bias_up = small_all[:, 8 * share : (8 + wide) * share].reshape(FF)
    full_out = unit(got_two, 0)
    full_up = jnp.concatenate([unit(got_two, 1 + c) for c in range(wide)], 1)
    full_down = got_two[:, (1 + wide) * share :].reshape(FF, D)

    prefix_len = jnp.sum(jnp.where(jnp.arange(prefix.shape[1]) == seq_slot, prefix, 0), 1)
    info = jnp.concatenate([first_block.astype(jnp.int32)[None], prefix_len.astype(jnp.int32)])

    tokens = inputs.reshape(micro * rows, D)
    grad_out = cotangent.reshape(micro * rows, D)
    values = tokens.astype(f32)
    normed_one, unit_one, inv_one = normalize(values, gain_one, shift_one)
    normed_low = normed_one.astype(bf16)
    queries = (product(normed_low, full_query) + bias_query).astype(bf16)
    key_local = product(normed_low, full_key).astype(bf16)
    value_local = (product(normed_low, full_value) + bias_value).astype(bf16)

    count = lax.axis_size("fsdp")
    pairs_up = [(i, i + 1) for i in range(0, count, 2)]
    pairs_down = [(i + 1, i) for i in range(0, count, 2)]

    def leading(array):
        return array.reshape(micro, rows, D)[:, :GLOBAL].reshape(micro * GLOBAL, D)

    lead = lax.ppermute(
        jnp.concatenate([leading(key_local), leading(value_local)], 1), "fsdp", pairs_up
    )
    attn_low, probs = attend(info, queries, key_local, value_local, lead, micro, rows)

    middle = values + product(attn_low, full_out) + bias_out
    normed_two, unit_two, inv_two = normalize(middle, gain_two, shift_two)
    normed_two_low = normed_two.astype(bf16)
    hidden = product(normed_two_low, full_up) + bias_up
    activated, gelu_back = jax.vjp(jax.nn.gelu, hidden)
    act_low = activated.astype(bf16)
    layer_out = (middle + product(act_low, full_down) + bias_down).astype(bf16)

    grad_outf = grad_out.astype(f32)
    grad_b_down = jnp.sum(grad_outf, 0)
    order_a, order_b = stage_orders()

    def by_owner(array):
        return array.reshape(n_dev, array.shape[0] // n_dev, D)

    grad_w_down = by_owner(product_w(act_low, grad_out))
    half = grad_w_down.shape[1] // 2
    down_a = scatter_sum(grad_w_down[:, :half], order_a)
    down_b = scatter_sum(grad_w_down[:, half:], order_b)
    d_act = product_t(grad_out, full_down)
    d_hidden = gelu_back(d_act)[0].astype(bf16)
    grad_b_up = jnp.sum(d_hidden, 0, dtype=f32)
    up_parts = [
        by_owner(product_w(normed_two_low, d_hidden[:, c * D : (c + 1) * D])) for c in range(wide)
    ]
    up_a = scatter_sum(jnp.concatenate(up_parts[: wide // 2], 1), order_a)
    up_b = scatter_sum(jnp.concatenate(up_parts[wide // 2 :], 1), order_b)
    d_normed_two = product_t(d_hidden, full_up)
    grad_gain_two = jnp.sum(d_normed_two * unit_two, 0)
    grad_shift_two = jnp.sum(d_normed_two, 0)
    d_middle = grad_outf + normalize_back(d_normed_two, unit_two, inv_two, gain_two)
    d_branch = d_middle.astype(bf16)
    grad_b_out = jnp.sum(d_branch, 0, dtype=f32)
    grad_w_out = by_owner(product_w(attn_low, d_branch))
    d_attended = product_t(d_branch, full_out).astype(bf16)

    d_queries, d_key, d_value, lead_k, lead_v = attend_back(
        queries, key_local, value_local, lead, d_attended, attn_low, probs, micro, rows
    )
    returned = lax.ppermute(jnp.concatenate([lead_k, lead_v], 1), "fsdp", pairs_down)
    returned = returned.astype(f32).reshape(micro, GLOBAL, 2 * D)
    extra = jnp.pad(returned, ((0, 0), (0, rows - GLOBAL), (0, 0))).reshape(micro * rows, 2 * D)
    d_keys = (d_key + extra[:, :D]).astype(bf16)
    d_values = (d_value + extra[:, D:]).astype(bf16)
    grad_b_query = jnp.sum(d_queries, 0, dtype=f32)
    grad_b_value = jnp.sum(d_values, 0, dtype=f32)
    out_and_query = jnp.concatenate([grad_w_out, by_owner(product_w(normed_low, d_queries))], 1)
    key_and_value = jnp.concatenate(
        [by_owner(product_w(normed_low, d_keys)), by_owner(product_w(normed_low, d_values))], 1
    )
    attn_a = scatter_sum(out_and_query, order_a)
    attn_b = scatter_sum(key_and_value, order_b)
    d_normed_one = (
        product_t(d_queries, full_query)
        + product_t(d_keys, full_key)
        + product_t(d_values, full_value)
    )
    grad_gain_one = jnp.sum(d_normed_one * unit_one, 0)
    grad_shift_one = jnp.sum(d_normed_one, 0)
    grad_inputs = d_middle + normalize_back(d_normed_one, unit_one, inv_one, gain_one)

    sums = jnp.stack(
        [
            grad_b_query, grad_b_value, grad_b_out, grad_b_down,
            grad_gain_one, grad_shift_one, grad_gain_two, grad_shift_two,
        ]
        + [grad_b_up[c * D : (c + 1) * D] for c in range(wide)]
    )
    sums = spread_sum(sums, order_a)
    owned = lax.dynamic_slice_in_dim(sums[:8], own * share, share, 1)
    owned_up = lax.dynamic_slice_in_dim(sums[8:].reshape(FF), own * share * wide, share * wide, 0)

    up_own = jnp.concatenate(
        [part[c * share : (c + 1) * share] for part in (up_a, up_b) for c in range(wide // 2)], 1
    )
    return (
        layer_out.reshape(micro, rows, D),
        grad_inputs.reshape(micro, rows, D),
        attn_a[share:],
        attn_b[:share],
        attn_b[share:],
        attn_a[:share],
        up_own,
        jnp.concatenate([down_a, down_b], 0),
        owned[0],
        owned[1],
        owned[2],
        owned_up,
        owned[3],
        owned[4],
        owned[5],
        owned[6],
        owned[7],
    )


def solution(mesh):
    tokens = P(None, BOTH, None)
    matrix = P(BOTH, None)
    line = P(BOTH)
    return jax.shard_map(
        body,
        mesh=mesh,
        in_specs=(tokens, tokens, P(None, "dp")) + (matrix,) * 6 + (line,) * 9,
        out_specs=(tokens, tokens) + (matrix,) * 6 + (line,) * 9,
        check_vma=False,
    )
```
